768 devices in a mesh: ctx: 48 (over z, y_lo), head: 16 (over y_hi, x, core).
Axes of the slice: x: 4, y: 8 (y_hi: 2, y_lo: 4; y = y_hi * 4 + y_lo), z: 12, core: 2. Of those that a mesh axis runs over, the one named last changes fastest.
Arguments:
- queries: bfloat16 [12288, 4096], P('ctx', 'head'), may hold values from -48 to 48
- enc_keys: bfloat16 [1536, 4096], P('ctx', 'head'), may hold values from -4 to 4
- enc_values: bfloat16 [1536, 4096], P('ctx', 'head'), may hold values from -6 to 6
- grad_out: bfloat16 [12288, 4096], P('ctx', 'head'), may hold values from -48 to 48
- out_weight: bfloat16 [4096, 4096], P('head'), may hold values from -0.09375 to 0.09375
Outputs:
- query_grad: bfloat16 [12288, 4096], P('ctx', 'head')
- key_grad: bfloat16 [1536, 4096], P('ctx', 'head')
- value_grad: bfloat16 [1536, 4096], P('ctx', 'head')
The draws below stay inside these ranges and needn't reach their ends.
All inputs are finite; a program needn't handle non-finite values.
Results may differ from the reference program's by a relative error of at most 0.0085.
Values may be sent and summed in bfloat16 or wider, within the bound.
No kernel may reach another device: no remote copies, remote signals or barrier semaphores. Data moves between devices by JAX's collectives and lax.ppermute only.
A program may use at most 64 MiB of HBM per device.

```python
import jax
import jax.numpy as jnp
from jax import lax

D = 4096
HEADS = 64
DH = 64
INNER = 4096
LQ = 12288
LK = 1536


def drawn_pair(key):
    query_key = jax.random.fold_in(key, 11)
    entry_key = jax.random.fold_in(key, 12)
    inner_width = HEADS * DH
    queries = jnp.clip(jax.random.normal(query_key, (LQ, inner_width), jnp.float32), -4.0, 4.0)
    keys_all = jnp.clip(jax.random.normal(entry_key, (LK, inner_width), jnp.float32), -4.0, 4.0)
    return (queries, keys_all)


def draw_queries(key, part):
    return drawn_pair(jax.random.fold_in(key, 7))[0].astype(jnp.bfloat16)


def draw_enc_keys(key, part):
    return drawn_pair(jax.random.fold_in(key, 7))[1].astype(jnp.bfloat16)


def block_scale(rng, extent, shards, smallest, largest):
    loudness = 1.0
    for position, shards_of in shards:
        heights = jax.random.uniform(jax.random.fold_in(jax.random.fold_in(rng, 6), position), (shards_of,), jnp.float32, smallest / len(shards), largest / len(shards))
        loudness = loudness * jnp.repeat(jnp.exp(heights), extent[position] // shards_of).reshape((-1,) + (1,) * (len(extent) - 1 - position))
    return loudness


def noise(rng, shape, deviation, reach, pieces=(), held_as=jnp.bfloat16):
    factor_of = block_scale(rng, shape, pieces, -0.22, 0.18) if pieces else 1.0
    values = jax.random.normal(rng, shape, jnp.float32) * deviation * factor_of
    return jnp.minimum(jnp.maximum(values, -reach), reach).astype(held_as)


def setup_inputs(seed: int = 0) -> dict:
    streams_of = jax.random.split(jax.random.key(seed), 6)
    return {
        "queries": draw_queries(jax.random.fold_in(streams_of[5], 71), 0),
        "enc_keys": draw_enc_keys(jax.random.fold_in(streams_of[5], 71), 0),
        "enc_values": noise(streams_of[2], (LK, INNER), 1.0, 6.0, ((0, 48), (1, 16))),
        "grad_out": noise(streams_of[3], (LQ, D), 8.0, 48.0, ((0, 48), (1, 16))),
        "out_weight": noise(streams_of[4], (INNER, D), D ** -0.5, 0.09375, ((0, 16),)),
    }


def by_head(array, length):
    return array.reshape(length, HEADS, DH).transpose(1, 0, 2)


def merged(array, length):
    return array.transpose(1, 0, 2).reshape(length, HEADS * DH).astype(jnp.bfloat16)


def reference(queries, enc_keys, enc_values, grad_out, out_weight):
    head_grads = jnp.dot(grad_out, out_weight.T, preferred_element_type=jnp.float32).astype(jnp.bfloat16)
    score_scale = DH ** -0.5

    def one_head(operands):
        query_head, key_head, value_head, grad_head = operands
        scores = score_scale * jnp.dot(query_head, key_head.T, preferred_element_type=jnp.float32)
        row_top = jnp.max(scores, axis=1, keepdims=True)
        exponent = jnp.exp(scores - row_top)
        attention = exponent / jnp.sum(exponent, axis=1, keepdims=True)
        attention_low = attention.astype(jnp.bfloat16)
        attended = jnp.dot(attention_low, value_head, preferred_element_type=jnp.float32)
        row_delta = jnp.sum(grad_head.astype(jnp.float32) * attended, axis=1, keepdims=True)
        prob_grad = jnp.dot(grad_head, value_head.T, preferred_element_type=jnp.float32)
        score_grad = (score_scale * attention * (prob_grad - row_delta)).astype(jnp.bfloat16)
        query_part = jnp.dot(score_grad, key_head, preferred_element_type=jnp.float32)
        key_part = jnp.dot(score_grad.T, query_head, preferred_element_type=jnp.float32)
        value_part = jnp.dot(attention_low.T, grad_head, preferred_element_type=jnp.float32)
        return query_part, key_part, value_part

    query_all, key_all, value_all = lax.map(
        one_head,
        (by_head(queries, LQ), by_head(enc_keys, LK), by_head(enc_values, LK), by_head(head_grads, LQ)),
    )
    return merged(query_all, LQ), merged(key_all, LK), merged(value_all, LK)
```

```python
import jax
import jax.numpy as jnp
from jax import lax
from jax.sharding import Mesh, PartitionSpec as P

DH = 64
BF = jnp.bfloat16
F32 = jnp.float32
Z, YL, YH, X, C = 12, 4, 2, 4, 2
CTX = ("z", "yl")
HEAD = ("yh", "x", "c")


def pack(block):
    rows = block.shape[0]
    return (
        block.reshape(2, rows // 2, YL, DH).transpose(2, 1, 0, 3).reshape(YL, rows // 2, 2 * DH)
    )


def unpack_rows(packed):
    n, half, _ = packed.shape
    return packed.reshape(n, half, 2, DH).transpose(0, 2, 1, 3).reshape(n * half * 2, DH)


def pack_rows(rows):
    half = rows.shape[0] // YL // 2
    return rows.reshape(YL, 2, half, DH).transpose(0, 2, 1, 3).reshape(YL, half, 2 * DH)


def unpack(packed):
    n, half, _ = packed.shape
    return packed.reshape(n, half, 2, DH).transpose(2, 1, 0, 3).reshape(2 * half, n * DH)


def exchange(block, axis):
    return lax.all_to_all(block, axis, 0, 0, tiled=True)


def local(queries, enc_keys, enc_values, grad_out, out_weight):
    rows, width = queries.shape
    keys_here = enc_keys.shape[0]
    key_count = keys_here * Z * YL
    other = lax.ppermute(grad_out, "yh", [(0, 1), (1, 0)])
    mine = lax.axis_index("yh")
    both = jnp.where(mine == 0, jnp.stack([grad_out, other]), jnp.stack([other, grad_out]))
    over_x = exchange(jnp.broadcast_to(both[None], (X,) + both.shape), "x")
    over_c = lax.ppermute(over_x, "c", [(0, 1), (1, 0)])
    core = lax.axis_index("c")
    weight = out_weight.reshape(width, YH, X, C, width)
    w_mine = lax.dynamic_index_in_dim(weight, core, 3, keepdims=False)
    w_other = lax.dynamic_index_in_dim(weight, 1 - core, 3, keepdims=False)
    head_grads = (
        jnp.einsum("xyrd,wyxd->rw", over_x, w_mine, preferred_element_type=F32)
        + jnp.einsum("xyrd,wyxd->rw", over_c, w_other, preferred_element_type=F32)
    ).astype(BF)

    q_packed = exchange(pack(queries), "yl")
    kv = jnp.concatenate(
        [enc_keys.reshape(keys_here, YL, DH), enc_values.reshape(keys_here, YL, DH)], axis=2
    ).transpose(1, 0, 2)
    kv_all = exchange(
        jnp.broadcast_to(kv[None], (Z,) + kv.shape).reshape(Z * YL, keys_here, 2 * DH), CTX
    ).reshape(key_count, 2 * DH)
    g_packed = exchange(pack(head_grads), "yl")

    q = unpack_rows(q_packed)
    g = unpack_rows(g_packed)
    k, v = kv_all[:, :DH], kv_all[:, DH:]
    scale = DH ** (-0.5)
    scores = scale * jnp.dot(q, k.T, preferred_element_type=F32)
    top = jnp.max(scores, axis=1, keepdims=True)
    exponent = jnp.exp(scores - top)
    attention = exponent / jnp.sum(exponent, axis=1, keepdims=True)
    low = attention.astype(BF)
    attended = jnp.dot(low, v, preferred_element_type=F32)
    delta = jnp.sum(g.astype(F32) * attended, axis=1, keepdims=True)
    prob_grad = jnp.dot(g, v.T, preferred_element_type=F32)
    score_grad = (scale * attention * (prob_grad - delta)).astype(BF)
    dq = jnp.dot(score_grad, k, preferred_element_type=F32).astype(BF)
    dk = jnp.dot(score_grad.T, q, preferred_element_type=F32)
    dv = jnp.dot(low.T, g, preferred_element_type=F32)
    dkv = jnp.concatenate([dk, dv], axis=1).astype(BF)

    dkv_parts = exchange(dkv.reshape(Z * YL, keys_here, 2 * DH), CTX)
    dkv_sum = jnp.sum(dkv_parts.reshape(Z, YL, keys_here, 2 * DH).astype(F32), axis=0).astype(BF)
    query_grad = unpack(exchange(pack_rows(dq), "yl"))
    heads_last = dkv_sum.transpose(1, 0, 2)
    key_grad = heads_last[:, :, :DH].reshape(keys_here, width)
    value_grad = heads_last[:, :, DH:].reshape(keys_here, width)
    return query_grad, key_grad, value_grad


def solution(mesh):
    fine = Mesh(mesh.devices.reshape(Z, YL, YH, X, C), CTX + HEAD)
    both = P(CTX, HEAD)
    return jax.shard_map(
        local,
        mesh=fine,
        in_specs=(both, both, both, both, P(HEAD, None)),
        out_specs=(both, both, both),
        check_vma=False,
    )
```
